32 devices in a mesh: feat: 8 (over z, y), ex: 4 (over x, core).
Axes of the slice: x: 2, y: 2, z: 4, core: 2. Of those that a mesh axis runs over, the one named last changes fastest.
Arguments:
- examples: bfloat16 [4096, 262144], P('ex', 'feat'), may hold values from -6 to 6
- weights: bfloat16 [262144], P('feat'), may hold values from -0.01171875 to 0.01171875
- labels: int32 [4096], P('ex'), may hold values from 0 to 1
- split: int32 [4096], P('ex'), may hold values 0 or 1
- val_weight: float32 [32, 4096], P(None, 'ex'), may hold values from 0.1 to 10
- strengths: float32 [256], replicated, may hold values from 0.05 to 1
- block_ids: int32 [262144], P('feat'), may hold values from 0 to 255
Outputs:
- solve: float32 [32, 262144], P(None, ('feat', 'ex'))
- hypergrad: float32 [32, 256], P(None, ('feat', 'ex'))
The draws below stay inside these ranges and needn't reach their ends.
All inputs are finite; a program needn't handle non-finite values. No bound on the sum of `split` on one device may be relied on, other than what follows from the above.
Results may differ from the reference program's by a relative error of at most 0.0029.
Values may be sent and summed in bfloat16 or wider, within the bound.
A program may use at most 128 MiB of HBM per device.

```python
import math
import jax
import jax.numpy as jnp
from jax import lax

F = 262144
NB = 256
R = 32
NEX = 4096


def set_ends(drawn, rng, smallest, high):
    longest = drawn.shape.index(max(drawn.shape))
    spots = []
    for shift in (0, 1):
        where = [jax.random.randint(jax.random.fold_in(rng, axis), (), 0, length) for axis, length in enumerate(drawn.shape)]
        where[longest] = (where[longest] + shift) % drawn.shape[longest]
        spots.append(tuple(where))
    return drawn.at[spots[0]].set(smallest).at[spots[1]].set(high)


def block_levels(key, shape, cuts, least, largest):
    def one(position, blocks):
        draws = jax.random.uniform(jax.random.fold_in(jax.random.fold_in(key, 6), position), (blocks,), jnp.float32, least / len(cuts), largest / len(cuts))
        return jnp.repeat(jnp.exp(draws), shape[position] // blocks).reshape((-1,) + (1,) * (len(shape) - position - 1))

    gain = one(*cuts[0])
    for cut in cuts[1:]:
        gain = gain * one(*cut)
    return gain


def gaussian(key, extent, scale, reach, shards=(), kind=jnp.bfloat16):
    array = scale * jax.random.normal(key, extent, jnp.float32)
    if shards:
        array = array * block_levels(key, extent, shards, -0.22, 0.18)
    return jnp.clip(array, -reach, reach).astype(kind)


def setup_inputs(seed: int = 0) -> dict:
    seeds = jax.random.split(jax.random.key(seed), 8)
    examples = gaussian(seeds[0], (NEX, F), 1.0, 6.0, ((0, 4), (1, 8)))
    weights = gaussian(seeds[1], (F,), F ** -0.5, 0.01171875, ((0, 8),))
    labels = set_ends(jax.random.randint(seeds[2], (NEX,), 0, 2), jax.random.fold_in(seeds[2], 1), 0, 1).astype(jnp.int32)
    split = set_ends((jax.random.randint(seeds[3], (NEX,), 0, 4) < 3).astype(jnp.int32), jax.random.fold_in(seeds[3], 1), 0, 1)
    val_weight = jnp.clip(jnp.exp(math.log(10.0) - 4.6051702 * jax.random.uniform(seeds[4], (R, NEX), jnp.float32) ** block_levels(seeds[4], (R, NEX), ((1, 4),), -0.2, 0.2)), 0.1, 10.0)
    strengths = jnp.clip(jnp.exp(jax.random.uniform(seeds[5], (NB,), jnp.float32, math.log(0.05), math.log(1.0))), 0.05, 1.0)
    block_ids = set_ends(jax.random.randint(seeds[6], (F,), 0, NB), jax.random.fold_in(seeds[6], 1), 0, NB - 1).astype(jnp.int32)
    return {"examples": examples, "weights": weights, "labels": labels, "split": split, "val_weight": val_weight, "strengths": strengths, "block_ids": block_ids}


def reference(examples, weights, labels, split, val_weight, strengths, block_ids):
    margin = jnp.dot(examples, weights, preferred_element_type=jnp.float32)
    prob = 1.0 / (1.0 + jnp.exp(-margin))
    train = split.astype(jnp.float32)
    curvew = train * prob * (1.0 - prob)
    err = (1.0 - train) * (prob - labels.astype(jnp.float32))
    gradw = (val_weight * err[None, :] / jnp.sqrt(jnp.float32(NEX))).astype(jnp.bfloat16)
    rhs = jnp.dot(gradw, examples, preferred_element_type=jnp.float32)
    lamf = strengths[block_ids]

    def apply_hessian(direc):
        dlow = direc.astype(jnp.bfloat16)
        tang = jnp.dot(dlow, examples.T, preferred_element_type=jnp.float32)
        wtang = (curvew[None, :] * tang).astype(jnp.bfloat16)
        prod = jnp.dot(wtang, examples, preferred_element_type=jnp.float32)
        return prod / jnp.float32(NEX) + lamf[None, :] * direc
    solve = jnp.zeros_like(rhs)
    resid = rhs
    direc = rhs
    norm_now = lax.optimization_barrier(jnp.sum(resid * resid, axis=1))
    for step in range(2):
        image = apply_hessian(direc)
        curv = lax.optimization_barrier(jnp.sum(direc * image, axis=1))
        alpha = norm_now / curv
        solve = solve + alpha[:, None] * direc
        resid = resid - alpha[:, None] * image
        if step == 0:
            norm_next = lax.optimization_barrier(jnp.sum(resid * resid, axis=1))
            direc = resid + (norm_next / norm_now)[:, None] * direc
            norm_now = norm_next
    product = solve * weights.astype(jnp.float32)[None, :]
    sums = jax.ops.segment_sum(product.T, block_ids, num_segments=NB).T
    return (solve, -strengths[None, :] * sums)
```

```python
import functools

import jax
import jax.numpy as jnp
from jax import lax
from jax.experimental import pallas as pl
from jax.experimental.pallas import tpu as pltpu
from jax.sharding import PartitionSpec as P

MESH = pl.DeviceIdType.MESH
VMEM = pl.BlockSpec(memory_space=pltpu.VMEM)
LANES = 128


def address(axis, pos):
    if axis == "feat":
        return (pos, lax.axis_index("ex"))
    return (lax.axis_index("feat"), pos)


def flip(pos, offset):
    out, mask = pos, 1
    while mask <= offset:
        if offset & mask:
            out = out + mask * (1 - 2 * lax.rem(lax.div(pos, mask), 2))
        mask *= 2
    return out


def meet(axis, peers):
    barrier = pltpu.get_barrier_semaphore()
    for peer in peers:
        pl.semaphore_signal(barrier, inc=1, device_id=address(axis, peer), device_id_type=MESH)
    pl.semaphore_wait(barrier, len(peers))


def total_kernel(axis, n, x_ref, out_ref, slots, send_sem, recv_sem):
    me = lax.axis_index(axis)
    peers = [lax.rem(me + k, n) for k in range(1, n)]
    meet(axis, peers)
    copies = []
    for k, peer in enumerate(peers):
        copy = pltpu.make_async_remote_copy(
            src_ref=x_ref,
            dst_ref=slots.at[k],
            send_sem=send_sem.at[k],
            recv_sem=recv_sem.at[k],
            device_id=address(axis, peer),
            device_id_type=MESH,
        )
        copy.start()
        copies.append(copy)
    total = x_ref[...]
    for k, copy in enumerate(copies):
        copy.wait_recv()
        total = total + slots[k]
    out_ref[...] = total
    for copy in copies:
        copy.wait_send()


def small_total(x, axis, ident):
    n = lax.axis_size(axis)
    if n == 1:
        return x
    return pl.pallas_call(
        functools.partial(total_kernel, axis, n),
        out_shape=jax.ShapeDtypeStruct(x.shape, x.dtype),
        in_specs=[VMEM],
        out_specs=VMEM,
        scratch_shapes=[
            pltpu.VMEM((n - 1,) + x.shape, x.dtype),
            pltpu.SemaphoreType.DMA((n - 1,)),
            pltpu.SemaphoreType.DMA((n - 1,)),
        ],
        compiler_params=pltpu.CompilerParams(collective_id=ident, has_side_effects=True),
    )(x)


def reduce_kernel(axis, n, x_ref, out_ref, slots, full, send_sem, recv_sem):
    me = lax.axis_index(axis)
    peers = [lax.rem(me + k, n) for k in range(1, n)]
    meet(axis, peers)
    first, second = [], []
    for k, peer in enumerate(peers):
        copy = pltpu.make_async_remote_copy(
            src_ref=x_ref.at[peer],
            dst_ref=slots.at[k],
            send_sem=send_sem.at[0, k],
            recv_sem=recv_sem.at[0, k],
            device_id=address(axis, peer),
            device_id_type=MESH,
        )
        copy.start()
        first.append(copy)
    total = x_ref[me]
    for k, copy in enumerate(first):
        copy.wait_recv()
        total = total + slots[k]
    full[me] = total
    for k, peer in enumerate(peers):
        copy = pltpu.make_async_remote_copy(
            src_ref=full.at[me],
            dst_ref=full.at[me],
            send_sem=send_sem.at[1, k],
            recv_sem=recv_sem.at[1, k],
            device_id=address(axis, peer),
            device_id_type=MESH,
        )
        copy.start()
        second.append(copy)
    for copy in second:
        copy.wait_recv()
    out_ref[...] = full[...]
    for copy in first + second:
        copy.wait_send()


def large_total(x, axis, ident):
    n = lax.axis_size(axis)
    if n == 1:
        return x
    rows = x.shape[0]
    y = x.reshape(n, rows // n, LANES)
    out = pl.pallas_call(
        functools.partial(reduce_kernel, axis, n),
        out_shape=jax.ShapeDtypeStruct(y.shape, y.dtype),
        in_specs=[VMEM],
        out_specs=VMEM,
        scratch_shapes=[
            pltpu.VMEM((n - 1,) + y.shape[1:], y.dtype),
            pltpu.VMEM(y.shape, y.dtype),
            pltpu.SemaphoreType.DMA((2, n - 1)),
            pltpu.SemaphoreType.DMA((2, n - 1)),
        ],
        compiler_params=pltpu.CompilerParams(collective_id=ident, has_side_effects=True),
    )(y)
    return out.reshape(rows, LANES)


def spread_kernel(n, share, based, *refs):
    if based:
        x_ref, base_ref, coef_ref, own_ref, all_ref = refs[:5]
    else:
        x_ref, own_ref, all_ref = refs[:3]
    acc, outbox, inbox, full, out_sem, in_sem, send_sem, recv_sem = refs[-8:]
    me = lax.axis_index("ex")
    masks = []
    while 2 ** len(masks) < n:
        masks.append(2 ** len(masks))
    meet("ex", [flip(me, mask) for mask in masks])

    copies = []
    slot = 0
    for level, mask in enumerate(masks):
        low = lax.rem(me, mask)
        bit = lax.rem(lax.div(me, mask), 2)
        groups = n // (2 * mask)
        upper = lax.div(me, 2 * mask)
        sent = []
        for k in range(groups):
            group = lax.rem(upper + 1 + k, groups) if groups > 1 else 0
            away = group * 2 * mask + (1 - bit) * mask + low
            kept = group * 2 * mask + bit * mask + low
            if level == 0:
                part = x_ref[:, pl.ds(pl.multiple_of(away * share, share), share)]
            else:
                part = acc[away]
            outbox[slot] = part.astype(jnp.bfloat16)
            copy = pltpu.make_async_remote_copy(
                src_ref=outbox.at[slot],
                dst_ref=inbox.at[slot],
                send_sem=out_sem.at[slot],
                recv_sem=in_sem.at[slot],
                device_id=address("ex", flip(me, mask)),
                device_id_type=MESH,
            )
            copy.start()
            sent.append((copy, kept, slot))
            slot += 1
        nexts = []
        for copy, kept, at in sent:
            if level == 0:
                mine = x_ref[:, pl.ds(pl.multiple_of(kept * share, share), share)]
            else:
                mine = acc[kept]
            nexts.append((copy, kept, at, mine))
        for copy, kept, at, mine in nexts:
            copy.wait_recv()
            acc[kept] = mine + inbox[at].astype(jnp.float32)
            copies.append(copy)
    own = acc[me] if n > 1 else x_ref[...]
    if based:
        own = base_ref[...] + coef_ref[:, 0:1] * own
    own_ref[...] = own
    full[me] = own.astype(jnp.bfloat16)

    ident = {}
    held = [0]
    order = []
    for mask in reversed(masks):
        for offset in held:
            ident[mask, offset] = len(ident)
        order.append((mask, list(held)))
        held = held + [mask ^ offset for offset in held]

    def passing(mask, offset):
        at = ident[mask, offset]
        chunk = flip(me, offset)
        return pltpu.make_async_remote_copy(
            src_ref=full.at[chunk],
            dst_ref=full.at[chunk],
            send_sem=send_sem.at[at],
            recv_sem=recv_sem.at[at],
            device_id=address("ex", flip(me, mask)),
            device_id_type=MESH,
        )

    live = {}
    for mask in reversed(masks):
        live[mask, 0] = passing(mask, 0)
        live[mask, 0].start()
    all_ref[:, pl.ds(pl.multiple_of(me * share, share), share)] = full[me]
    for mask, offsets in order:
        for offset in offsets:
            live[mask, offset].wait_recv()
            arrived = mask ^ offset
            for smaller in reversed(masks):
                if smaller < mask:
                    live[smaller, arrived] = passing(smaller, arrived)
                    live[smaller, arrived].start()
            chunk = flip(me, arrived)
            all_ref[:, pl.ds(pl.multiple_of(chunk * share, share), share)] = full[chunk]
    for copy in copies:
        copy.wait_send()
    for copy in live.values():
        copy.wait_send()


def spread(x, base, coef, ident):
    n = lax.axis_size("ex")
    rows, width = x.shape
    share = width // n
    based = base is not None
    count = max(n - 1, 1)
    return pl.pallas_call(
        functools.partial(spread_kernel, n, share, based),
        out_shape=(
            jax.ShapeDtypeStruct((rows, share), jnp.float32),
            jax.ShapeDtypeStruct((rows, width), jnp.bfloat16),
        ),
        in_specs=[VMEM] * (3 if based else 1),
        out_specs=(VMEM, VMEM),
        scratch_shapes=[
            pltpu.VMEM((n, rows, share), jnp.float32),
            pltpu.VMEM((count, rows, share), jnp.bfloat16),
            pltpu.VMEM((count, rows, share), jnp.bfloat16),
            pltpu.VMEM((n, rows, share), jnp.bfloat16),
        ]
        + [pltpu.SemaphoreType.DMA((count,))] * 4,
        compiler_params=pltpu.CompilerParams(collective_id=ident, has_side_effects=True),
    )(*((x, base, coef) if based else (x,)))


def to_rows(x):
    rows, cols = x.shape
    if cols % LANES == 0:
        return x.reshape(rows, cols // LANES, LANES).transpose(1, 0, 2).reshape(-1, LANES)
    flat = x.reshape(-1)
    return jnp.pad(flat, (0, -flat.shape[0] % LANES)).reshape(-1, LANES)


def from_rows(x, shape):
    rows, cols = shape
    if cols % LANES == 0:
        return x.reshape(cols // LANES, rows, LANES).transpose(1, 0, 2).reshape(rows, cols)
    return x.reshape(-1)[: rows * cols].reshape(rows, cols)


def pack(arrays, multiple):
    out = jnp.concatenate([to_rows(x) for x in arrays], axis=0)
    return jnp.pad(out, ((0, -out.shape[0] % multiple), (0, 0)))


def unpack(x, arrays):
    out, at = [], 0
    for like in arrays:
        count = -(-like.shape[0] * like.shape[1] // LANES)
        out.append(from_rows(x[at : at + count], like.shape))
        at += count
    return out


def shards(examples, weights, labels, split, val_weight, strengths, block_ids):
    n_ex = lax.axis_size("ex")
    n_feat = lax.axis_size("feat")
    ex_pos = lax.axis_index("ex")
    feat_pos = lax.axis_index("feat")
    total = examples.shape[0] * n_ex
    width = examples.shape[1]
    share = width // n_ex
    blocks = strengths.shape[0]
    nb_feat = blocks // n_feat
    nb_local = nb_feat // n_ex
    start = ex_pos * share

    def reduced(x, pieces):
        parts = []
        for _ in range(pieces):
            part = lax.reduce_precision(x, 8, 7)
            parts.append(part.astype(jnp.bfloat16))
            x = x - part
        return parts

    part = jnp.dot(examples, weights, preferred_element_type=jnp.float32)
    (margin,) = unpack(small_total(pack([part[None, :]], 8), "feat", 0), [part[None, :]])
    margin = margin[0]
    prob = 1.0 / (1.0 + jnp.exp(-margin))
    train = split.astype(jnp.float32)
    curvew = train * prob * (1.0 - prob)
    err = (1.0 - train) * (prob - labels.astype(jnp.float32))
    gradw = (val_weight * err[None, :] / jnp.sqrt(jnp.float32(total))).astype(jnp.bfloat16)
    rhs, low = spread(jnp.dot(gradw, examples, preferred_element_type=jnp.float32), None, None, 1)

    ids_loc = lax.dynamic_slice_in_dim(block_ids, start, share, 0)
    w_loc = lax.dynamic_slice_in_dim(weights, start, share, 0).astype(jnp.float32)
    onehot = (ids_loc[:, None] == jnp.arange(blocks, dtype=jnp.int32)[None, :]).astype(jnp.bfloat16)
    levels = jnp.stack(reduced(strengths, 3), axis=0)
    lam = jnp.sum(
        lax.dot_general(levels, onehot, (((1,), (1,)), ((), ())), preferred_element_type=jnp.float32),
        axis=0,
    )

    def tangents(direc):
        return lax.dot_general(
            direc, examples, (((1,), (1,)), ((), ())), preferred_element_type=jnp.float32
        )

    scaled = lam[None, :] * rhs
    sums = jnp.stack([jnp.sum(rhs * rhs, axis=1), jnp.sum(scaled * rhs, axis=1)])
    part = tangents(low)
    tang, sums = unpack(large_total(pack([part, sums], 8 * n_feat), "feat", 2), [part, sums])
    weighted = curvew[None, :] * tang
    sums = jnp.concatenate([sums, jnp.sum(weighted * tang, axis=1)[None, :]])
    (sums,) = unpack(small_total(pack([sums], 8), "ex", 3), [sums])
    norm_now, damp, along = sums[0], sums[1], sums[2]
    alpha = norm_now / (along / jnp.float32(total) + damp)

    prod = jnp.dot(weighted.astype(jnp.bfloat16), examples, preferred_element_type=jnp.float32)
    coef = jnp.broadcast_to((-alpha / jnp.float32(total))[:, None], (alpha.shape[0], LANES))
    resid, low = spread(prod, rhs - alpha[:, None] * scaled, coef, 4)

    stepped = lam[None, :] * resid
    sums = jnp.stack(
        [
            jnp.sum(resid * resid, axis=1),
            jnp.sum(stepped * resid, axis=1),
            jnp.sum(stepped * rhs, axis=1),
        ]
    )
    both = jnp.concatenate([rhs, resid]) * w_loc[None, :]
    pieces = jnp.concatenate(reduced(both, 2))
    rows = both.shape[0]
    grouped = jnp.dot(pieces, onehot, preferred_element_type=jnp.float32)
    grouped = grouped[:rows] + grouped[rows:]
    part = tangents(low)
    parts = [part, grouped, sums]
    turned, grouped, sums = unpack(large_total(pack(parts, 8 * n_feat), "feat", 5), parts)
    grouped = lax.dynamic_slice_in_dim(grouped, feat_pos * nb_feat, nb_feat, 1)
    heavy = curvew[None, :] * turned
    sums = jnp.concatenate(
        [sums, jnp.sum(heavy * turned, axis=1)[None, :], jnp.sum(heavy * tang, axis=1)[None, :]]
    )
    parts = [grouped, sums]
    grouped, sums = unpack(small_total(pack(parts, 8), "ex", 6), parts)
    norm_next = sums[0]
    beta = norm_next / norm_now
    curved = sums[3] + 2.0 * beta * sums[4] + beta * beta * along
    damped = sums[1] + 2.0 * beta * sums[2] + beta * beta * damp
    step = norm_next / (curved / jnp.float32(total) + damped)
    first = alpha + step * beta
    solve = first[:, None] * rhs + step[:, None] * resid
    grouped = lax.dynamic_slice_in_dim(grouped, ex_pos * nb_local, nb_local, 1)
    half = rows // 2
    block_sums = first[:, None] * grouped[:half] + step[:, None] * grouped[half:]
    own = lax.dynamic_slice_in_dim(
        strengths, (feat_pos * n_ex + ex_pos) * nb_local, nb_local, 0
    )
    return (solve, -own[None, :] * block_sums)


def solution(mesh):
    placed = (P("ex", "feat"), P("feat"), P("ex"), P("ex"), P(None, "ex"), P(), P("feat"))
    return jax.shard_map(
        shards,
        mesh=mesh,
        in_specs=placed,
        out_specs=(P(None, ("feat", "ex")), P(None, ("feat", "ex"))),
        check_vma=False,
    )
```

```python
import functools

import jax
import jax.numpy as jnp
from jax import lax
from jax.experimental import pallas as pl
from jax.experimental.pallas import tpu as pltpu
from jax.sharding import PartitionSpec as P

MESH = pl.DeviceIdType.MESH
VMEM = pl.BlockSpec(memory_space=pltpu.VMEM)
LANES = 128


def address(axis, pos):
    if axis == "feat":
        return (pos, lax.axis_index("ex"))
    return (lax.axis_index("feat"), pos)


def flip(pos, offset):
    out, mask = pos, 1
    while mask <= offset:
        if offset & mask:
            out = out + mask * (1 - 2 * lax.rem(lax.div(pos, mask), 2))
        mask *= 2
    return out


def meet(axis, peers):
    barrier = pltpu.get_barrier_semaphore()
    for peer in peers:
        pl.semaphore_signal(barrier, inc=1, device_id=address(axis, peer), device_id_type=MESH)
    pl.semaphore_wait(barrier, len(peers))


def total_kernel(axis, n, x_ref, out_ref, slots, send_sem, recv_sem):
    me = lax.axis_index(axis)
    peers = [lax.rem(me + k, n) for k in range(1, n)]
    meet(axis, peers)
    copies = []
    for k, peer in enumerate(peers):
        copy = pltpu.make_async_remote_copy(
            src_ref=x_ref,
            dst_ref=slots.at[k],
            send_sem=send_sem.at[k],
            recv_sem=recv_sem.at[k],
            device_id=address(axis, peer),
            device_id_type=MESH,
        )
        copy.start()
        copies.append(copy)
    total = x_ref[...]
    for k, copy in enumerate(copies):
        copy.wait_recv()
        total = total + slots[k]
    out_ref[...] = total
    for copy in copies:
        copy.wait_send()


def small_total(x, axis, ident):
    n = lax.axis_size(axis)
    if n == 1:
        return x
    return pl.pallas_call(
        functools.partial(total_kernel, axis, n),
        out_shape=jax.ShapeDtypeStruct(x.shape, x.dtype),
        in_specs=[VMEM],
        out_specs=VMEM,
        scratch_shapes=[
            pltpu.VMEM((n - 1,) + x.shape, x.dtype),
            pltpu.SemaphoreType.DMA((n - 1,)),
            pltpu.SemaphoreType.DMA((n - 1,)),
        ],
        compiler_params=pltpu.CompilerParams(collective_id=ident, has_side_effects=True),
    )(x)


def reduce_kernel(axis, n, x_ref, out_ref, slots, full, send_sem, recv_sem):
    me = lax.axis_index(axis)
    peers = [lax.rem(me + k, n) for k in range(1, n)]
    meet(axis, peers)
    first, second = [], []
    for k, peer in enumerate(peers):
        copy = pltpu.make_async_remote_copy(
            src_ref=x_ref.at[peer],
            dst_ref=slots.at[k],
            send_sem=send_sem.at[0, k],
            recv_sem=recv_sem.at[0, k],
            device_id=address(axis, peer),
            device_id_type=MESH,
        )
        copy.start()
        first.append(copy)
    total = x_ref[me]
    for k, copy in enumerate(first):
        copy.wait_recv()
        total = total + slots[k]
    full[me] = total
    for k, peer in enumerate(peers):
        copy = pltpu.make_async_remote_copy(
            src_ref=full.at[me],
            dst_ref=full.at[me],
            send_sem=send_sem.at[1, k],
            recv_sem=recv_sem.at[1, k],
            device_id=address(axis, peer),
            device_id_type=MESH,
        )
        copy.start()
        second.append(copy)
    for copy in second:
        copy.wait_recv()
    out_ref[...] = full[...]
    for copy in first + second:
        copy.wait_send()


def large_total(x, axis, ident):
    n = lax.axis_size(axis)
    if n == 1:
        return x
    rows = x.shape[0]
    y = x.reshape(n, rows // n, LANES)
    out = pl.pallas_call(
        functools.partial(reduce_kernel, axis, n),
        out_shape=jax.ShapeDtypeStruct(y.shape, y.dtype),
        in_specs=[VMEM],
        out_specs=VMEM,
        scratch_shapes=[
            pltpu.VMEM((n - 1,) + y.shape[1:], y.dtype),
            pltpu.VMEM(y.shape, y.dtype),
            pltpu.SemaphoreType.DMA((2, n - 1)),
            pltpu.SemaphoreType.DMA((2, n - 1)),
        ],
        compiler_params=pltpu.CompilerParams(collective_id=ident, has_side_effects=True),
    )(y)
    return out.reshape(rows, LANES)


def spread_kernel(n, share, pieces, based, *refs):
    if based:
        x_ref, base_ref, coef_ref, own_ref, all_ref = refs[:5]
    else:
        x_ref, own_ref, all_ref = refs[:3]
    scratch = refs[-8:]
    me = lax.axis_index("ex")
    masks = []
    while 2 ** len(masks) < n:
        masks.append(2 ** len(masks))
    meet("ex", [flip(me, mask) for mask in masks])
    if based:
        ends = (base_ref, coef_ref, own_ref, all_ref)
    else:
        ends = (None, None, own_ref, all_ref)
    lanes = [
        spread_piece(n, share, share // pieces, piece, masks, x_ref, ends, *[r.at[piece] for r in scratch])
        for piece in range(pieces)
    ]
    while lanes:
        lanes = [lane for lane in lanes if next(lane, None)]


def spread_piece(n, share, size, piece, masks, x_ref, ends, acc, outbox, inbox, full, out_sem, in_sem, send_sem, recv_sem):
    base_ref, coef_ref, own_ref, all_ref = ends
    me = lax.axis_index("ex")

    def columns(chunk):
        return pl.ds(pl.multiple_of(chunk * share + piece * size, LANES), size)

    here = pl.ds(piece * size, size)
    copies = []
    slot = 0
    for level, mask in enumerate(masks):
        low = lax.rem(me, mask)
        bit = lax.rem(lax.div(me, mask), 2)
        groups = n // (2 * mask)
        upper = lax.div(me, 2 * mask)
        sent = []
        for k in range(groups):
            group = lax.rem(upper + 1 + k, groups) if groups > 1 else 0
            away = group * 2 * mask + (1 - bit) * mask + low
            kept = group * 2 * mask + bit * mask + low
            if level == 0:
                part = x_ref[:, columns(away)]
            else:
                part = acc[away]
            outbox[slot] = part.astype(jnp.bfloat16)
            copy = pltpu.make_async_remote_copy(
                src_ref=outbox.at[slot],
                dst_ref=inbox.at[slot],
                send_sem=out_sem.at[slot],
                recv_sem=in_sem.at[slot],
                device_id=address("ex", flip(me, mask)),
                device_id_type=MESH,
            )
            copy.start()
            sent.append((copy, kept, slot))
            slot += 1
        yield True
        nexts = []
        for copy, kept, at in sent:
            if level == 0:
                mine = x_ref[:, columns(kept)]
            else:
                mine = acc[kept]
            nexts.append((copy, kept, at, mine))
        for copy, kept, at, mine in nexts:
            copy.wait_recv()
            acc[kept] = mine + inbox[at].astype(jnp.float32)
            copies.append(copy)
    own = acc[me] if n > 1 else x_ref[:, here]
    if base_ref is not None:
        own = base_ref[:, here] + coef_ref[:, 0:1] * own
    own_ref[:, here] = own
    full[me] = own.astype(jnp.bfloat16)

    ident = {}
    held = [0]
    order = []
    for mask in reversed(masks):
        for offset in held:
            ident[mask, offset] = len(ident)
        order.append((mask, list(held)))
        held = held + [mask ^ offset for offset in held]

    def passing(mask, offset):
        at = ident[mask, offset]
        chunk = flip(me, offset)
        return pltpu.make_async_remote_copy(
            src_ref=full.at[chunk],
            dst_ref=full.at[chunk],
            send_sem=send_sem.at[at],
            recv_sem=recv_sem.at[at],
            device_id=address("ex", flip(me, mask)),
            device_id_type=MESH,
        )

    live = {}
    for mask in reversed(masks):
        live[mask, 0] = passing(mask, 0)
        live[mask, 0].start()
    all_ref[:, columns(me)] = full[me]
    for mask, offsets in order:
        yield True
        for offset in offsets:
            live[mask, offset].wait_recv()
            arrived = mask ^ offset
            for smaller in reversed(masks):
                if smaller < mask:
                    live[smaller, arrived] = passing(smaller, arrived)
                    live[smaller, arrived].start()
            chunk = flip(me, arrived)
            all_ref[:, columns(chunk)] = full[chunk]
    yield True
    for copy in copies:
        copy.wait_send()
    for copy in live.values():
        copy.wait_send()


def spread(x, base, coef, ident):
    n = lax.axis_size("ex")
    rows, width = x.shape
    share = width // n
    based = base is not None
    count = max(n - 1, 1)
    pieces = 4 if share % (4 * LANES) == 0 else 1
    size = share // pieces
    return pl.pallas_call(
        functools.partial(spread_kernel, n, share, pieces, based),
        out_shape=(
            jax.ShapeDtypeStruct((rows, share), jnp.float32),
            jax.ShapeDtypeStruct((rows, width), jnp.bfloat16),
        ),
        in_specs=[VMEM] * (3 if based else 1),
        out_specs=(VMEM, VMEM),
        scratch_shapes=[
            pltpu.VMEM((pieces, n, rows, size), jnp.float32),
            pltpu.VMEM((pieces, count, rows, size), jnp.bfloat16),
            pltpu.VMEM((pieces, count, rows, size), jnp.bfloat16),
            pltpu.VMEM((pieces, n, rows, size), jnp.bfloat16),
        ]
        + [pltpu.SemaphoreType.DMA((pieces, count))] * 4,
        compiler_params=pltpu.CompilerParams(collective_id=ident, has_side_effects=True),
    )(*((x, base, coef) if based else (x,)))


def to_rows(x):
    rows, cols = x.shape
    if cols % LANES == 0:
        return x.reshape(rows, cols // LANES, LANES).transpose(1, 0, 2).reshape(-1, LANES)
    flat = x.reshape(-1)
    return jnp.pad(flat, (0, -flat.shape[0] % LANES)).reshape(-1, LANES)


def from_rows(x, shape):
    rows, cols = shape
    if cols % LANES == 0:
        return x.reshape(cols // LANES, rows, LANES).transpose(1, 0, 2).reshape(rows, cols)
    return x.reshape(-1)[: rows * cols].reshape(rows, cols)


def pack(arrays, multiple):
    out = jnp.concatenate([to_rows(x) for x in arrays], axis=0)
    return jnp.pad(out, ((0, -out.shape[0] % multiple), (0, 0)))


def unpack(x, arrays):
    out, at = [], 0
    for like in arrays:
        count = -(-like.shape[0] * like.shape[1] // LANES)
        out.append(from_rows(x[at : at + count], like.shape))
        at += count
    return out


def shards(examples, weights, labels, split, val_weight, strengths, block_ids):
    n_ex = lax.axis_size("ex")
    n_feat = lax.axis_size("feat")
    ex_pos = lax.axis_index("ex")
    feat_pos = lax.axis_index("feat")
    total = examples.shape[0] * n_ex
    width = examples.shape[1]
    share = width // n_ex
    blocks = strengths.shape[0]
    nb_feat = blocks // n_feat
    nb_local = nb_feat // n_ex
    start = ex_pos * share

    def reduced(x, pieces):
        parts = []
        for _ in range(pieces):
            part = lax.reduce_precision(x, 8, 7)
            parts.append(part.astype(jnp.bfloat16))
            x = x - part
        return parts

    part = jnp.dot(examples, weights, preferred_element_type=jnp.float32)
    (margin,) = unpack(small_total(pack([part[None, :]], 8), "feat", 0), [part[None, :]])
    margin = margin[0]
    prob = 1.0 / (1.0 + jnp.exp(-margin))
    train = split.astype(jnp.float32)
    curvew = train * prob * (1.0 - prob)
    err = (1.0 - train) * (prob - labels.astype(jnp.float32))
    gradw = (val_weight * err[None, :] / jnp.sqrt(jnp.float32(total))).astype(jnp.bfloat16)
    rhs, low = spread(jnp.dot(gradw, examples, preferred_element_type=jnp.float32), None, None, 1)

    ids_loc = lax.dynamic_slice_in_dim(block_ids, start, share, 0)
    w_loc = lax.dynamic_slice_in_dim(weights, start, share, 0).astype(jnp.float32)
    onehot = (ids_loc[:, None] == jnp.arange(blocks, dtype=jnp.int32)[None, :]).astype(jnp.bfloat16)
    levels = jnp.stack(reduced(strengths, 3), axis=0)
    lam = jnp.sum(
        lax.dot_general(levels, onehot, (((1,), (1,)), ((), ())), preferred_element_type=jnp.float32),
        axis=0,
    )

    def tangents(direc):
        return lax.dot_general(
            direc, examples, (((1,), (1,)), ((), ())), preferred_element_type=jnp.float32
        )

    scaled = lam[None, :] * rhs
    sums = jnp.stack([jnp.sum(rhs * rhs, axis=1), jnp.sum(scaled * rhs, axis=1)])
    part = tangents(low)
    tang, sums = unpack(large_total(pack([part, sums], 8 * n_feat), "feat", 2), [part, sums])
    weighted = curvew[None, :] * tang
    sums = jnp.concatenate([sums, jnp.sum(weighted * tang, axis=1)[None, :]])
    (sums,) = unpack(small_total(pack([sums], 8), "ex", 3), [sums])
    norm_now, damp, along = sums[0], sums[1], sums[2]
    alpha = norm_now / (along / jnp.float32(total) + damp)

    prod = jnp.dot(weighted.astype(jnp.bfloat16), examples, preferred_element_type=jnp.float32)
    coef = jnp.broadcast_to((-alpha / jnp.float32(total))[:, None], (alpha.shape[0], LANES))
    resid, low = spread(prod, rhs - alpha[:, None] * scaled, coef, 4)

    stepped = lam[None, :] * resid
    sums = jnp.stack(
        [
            jnp.sum(resid * resid, axis=1),
            jnp.sum(stepped * resid, axis=1),
            jnp.sum(stepped * rhs, axis=1),
        ]
    )
    both = jnp.concatenate([rhs, resid]) * w_loc[None, :]
    pieces = jnp.concatenate(reduced(both, 2))
    rows = both.shape[0]
    grouped = jnp.dot(pieces, onehot, preferred_element_type=jnp.float32)
    grouped = grouped[:rows] + grouped[rows:]
    part = tangents(low)
    parts = [part, grouped, sums]
    turned, grouped, sums = unpack(large_total(pack(parts, 8 * n_feat), "feat", 5), parts)
    grouped = lax.dynamic_slice_in_dim(grouped, feat_pos * nb_feat, nb_feat, 1)
    heavy = curvew[None, :] * turned
    sums = jnp.concatenate(
        [sums, jnp.sum(heavy * turned, axis=1)[None, :], jnp.sum(heavy * tang, axis=1)[None, :]]
    )
    parts = [grouped, sums]
    grouped, sums = unpack(small_total(pack(parts, 8), "ex", 6), parts)
    norm_next = sums[0]
    beta = norm_next / norm_now
    curved = sums[3] + 2.0 * beta * sums[4] + beta * beta * along
    damped = sums[1] + 2.0 * beta * sums[2] + beta * beta * damp
    step = norm_next / (curved / jnp.float32(total) + damped)
    first = alpha + step * beta
    solve = first[:, None] * rhs + step[:, None] * resid
    grouped = lax.dynamic_slice_in_dim(grouped, ex_pos * nb_local, nb_local, 1)
    half = rows // 2
    block_sums = first[:, None] * grouped[:half] + step[:, None] * grouped[half:]
    own = lax.dynamic_slice_in_dim(
        strengths, (feat_pos * n_ex + ex_pos) * nb_local, nb_local, 0
    )
    return (solve, -own[None, :] * block_sums)


def solution(mesh):
    placed = (P("ex", "feat"), P("feat"), P("ex"), P("ex"), P(None, "ex"), P(), P("feat"))
    return jax.shard_map(
        shards,
        mesh=mesh,
        in_specs=placed,
        out_specs=(P(None, ("feat", "ex")), P(None, ("feat", "ex"))),
        check_vma=False,
    )
```
